32 devices in a mesh: ty: 4 (over y, x), tx: 8 (over z, core).
Axes of the slice: x: 2, y: 2, z: 4, core: 2. Of those that a mesh axis runs over, the one named last changes fastest.
Arguments:
- block_sums: float32 [4096, 1, 1024], P(('ty', 'tx')), may hold values from -6 to 6
- block_weights: float32 [4096, 1, 1024], P(('ty', 'tx')), may hold values from 0.1 to 2
- block_tile: int32 [4096, 1], P(('ty', 'tx')), may hold values from 0 to 31; in each aligned block of 128 rows (0 to 127, 128 to 255, ...) at most 8 rows name the same one
- block_row: int32 [4096], P(('ty', 'tx')), may hold values from 0 to 127
- prior_weight: float32 [512, 8192], P('ty', 'tx'), may hold values from 0.1 to 1
Outputs:
- solution_field: float32 [512, 8192], P('ty', 'tx')
- residual: float32 [512, 8192], P('ty', 'tx')
The draws below stay inside these ranges and needn't reach their ends.
Inputs may be any that keep to these rules, and one draw needn't show every extreme that they name: `block_tile`: among the 128 blocks of one log shard no tile is named more than 8 times, a bound that some block reaches.
All inputs are finite; a program needn't handle non-finite values.
Results may differ from the reference program's by a relative error of at most 0.0003.
Values sent between devices are 32-bit elements; how exact they have to be, the bound alone decides.
A program may use at most 64 MiB of HBM per device.

```python
import math
import jax
import jax.numpy as jnp
import numpy as np
from jax import lax

ROWS = 128
COLS = 1024
HALF = 32
ITERS = 2
BLK_DEV = 128
BAND = 1
CAP = 8
BLOCKS = 4096
NY = 512
NX = 8192
N_TX = 8
DEVICES = 32


def set_ends(drawn, rng, least, top_value):
    extent = drawn.shape
    index_at = [jax.random.randint(jax.random.fold_in(rng, axis), (), 0, extent[axis]) for axis in range(len(extent))]
    drawn = drawn.at[tuple(index_at)].set(least)
    longest = extent.index(max(extent))
    index_at[longest] = (index_at[longest] + 1) % extent[longest]
    return drawn.at[tuple(index_at)].set(top_value)


def steps_of(stream_key, shape, cuts, smallest, top_value):
    level = 1.0
    for axis_at, parts in cuts:
        heights = jax.random.uniform(jax.random.fold_in(jax.random.fold_in(stream_key, 6), axis_at), (parts,), jnp.float32, smallest / len(cuts), top_value / len(cuts))
        level = level * jnp.repeat(jnp.exp(heights), shape[axis_at] // parts).reshape((-1,) + (1,) * (len(shape) - 1 - axis_at))
    return level


def assign_block(rng, own, number, rows, count, top, limit, slope):
    sequence = jax.random.permutation(rng, count)
    packed, ordinary = portions_of(count, rows * top, limit, slope, True), portions_of(count, rows * top, limit, slope, False)
    places = jnp.arange(count)

    def named(sizes, rotation):
        used = int((sizes > 0).sum())
        fixed = max(1, used // 4)
        passed = fixed + (places - fixed + rotation * (used - fixed)) % max(1, count - fixed)
        return jnp.zeros((count,), jnp.int32).at[sequence[jnp.where(places < fixed, places, passed)]].set(jnp.asarray(sizes, jnp.int32))

    sizes = jnp.where(number % 4 == 0, named(packed, number // 4), named(ordinary, number - number // 4 - 1))
    mixed = jax.random.permutation(jax.random.fold_in(own, 3), count)
    giver, receiver = mixed[0:count // 2 * 2:2], mixed[1:count // 2 * 2:2]
    slack = jnp.minimum(sizes[giver] - 1, limit - sizes[receiver]) // 2
    slack = jnp.where((giver == sequence[0]) | (receiver == sequence[0]) | (sizes[receiver] == 0), 0, jnp.maximum(slack, 0))
    passed = jax.random.randint(jax.random.fold_in(own, 4), (count // 2,), 0, 1 << 20) % (slack + 1)
    sizes = sizes.at[giver].add(-passed).at[receiver].add(passed)
    members = jnp.searchsorted(jnp.cumsum(sizes), jnp.arange(rows * top), side="right").astype(jnp.int32)
    listing = members.reshape(top, rows).T
    listing = listing[jax.random.permutation(jax.random.fold_in(own, 1), rows)]
    rotation = jax.random.randint(jax.random.fold_in(own, 2), (rows, 1), 0, top)
    return jnp.take_along_axis(listing, (jnp.arange(top)[None, :] + rotation) % top, axis=1)


def portions_of(number_of, total, reach, slope, full):
    portions = [(1 << 20) // math.isqrt(rank ** slope) + 1 for rank in range(1, number_of + 1)]
    largest = reach if full else min(reach, max(-(-total // number_of), total * portions[0] // sum(portions)))
    least = 1 if total - largest >= number_of - 1 else 0
    holding, surplus = [largest] + [least] * (number_of - 1), total - largest - least * (number_of - 1)
    while surplus > 0:
        candidates = [i for i in range(1, number_of) if holding[i] < largest] or [i for i in range(1, number_of) if holding[i] < reach]
        whole, remaining = sum([portions[i] for i in candidates]), surplus
        for i in candidates:
            more = min(reach - holding[i], max(1, remaining * portions[i] // whole), surplus)
            holding[i] = holding[i] + more
            surplus = surplus - more
    return np.array(holding)


def noise(key, shape, scale, limit, pieces=(), held_as=jnp.bfloat16):
    array = scale * jax.random.normal(key, shape, jnp.float32)
    if pieces:
        array = array * steps_of(key, shape, pieces, -0.22, 0.18)
    return jnp.clip(array, -limit, limit).astype(held_as)


def setup_inputs(seed: int = 0) -> dict:
    streams_of = jax.random.split(jax.random.key(seed), 6)
    block_sums = noise(streams_of[0], (BLOCKS, BAND, COLS), 1.0, 6.0, ((0, 32),), jnp.float32)
    block_weights = jnp.clip(jnp.exp(math.log(2.0) - 2.9957323 * jax.random.uniform(streams_of[1], (BLOCKS, BAND, COLS), jnp.float32) ** steps_of(streams_of[1], (BLOCKS, BAND, COLS), ((0, 32),), -0.2, 0.2)), 0.1, 2.0)
    block_tile_keys = jax.random.split(jax.random.fold_in(streams_of[2], 1), BLOCKS // BLK_DEV)
    block_tile_turns = jax.random.permutation(jax.random.fold_in(streams_of[2], 3), BLOCKS // BLK_DEV)
    block_tile = jax.vmap(lambda own, number: assign_block(jax.random.fold_in(streams_of[2], 2), own, number, BLK_DEV, DEVICES, 1, CAP, 2))(block_tile_keys, block_tile_turns).reshape((BLOCKS, 1))
    block_row = set_ends(jax.random.randint(streams_of[3], (BLOCKS,), 0, BLK_DEV), jax.random.fold_in(streams_of[3], 1), 0, BLK_DEV - 1).astype(jnp.int32)
    prior_weight = jnp.clip(jnp.exp(math.log(1.0) - 2.3025851 * jax.random.uniform(streams_of[4], (NY, NX), jnp.float32) ** steps_of(streams_of[4], (NY, NX), ((0, 4), (1, 8)), -0.2, 0.2)), 0.1, 1.0)
    return dict(block_sums=block_sums, block_weights=block_weights, block_tile=block_tile, block_row=block_row, prior_weight=prior_weight)


def kernel_taps():
    dist = jnp.abs(jnp.arange(-HALF, HALF + 1).astype(jnp.float32))
    scaled = dist / (HALF + 1.0)
    taps = (1.0 - scaled) ** 4 * (1.0 + 4.0 * scaled)
    return taps / jnp.sum(taps)

def smooth(field, taps):
    image = field[None, None]
    image = lax.conv_general_dilated(image, taps[None, None, :, None], (1, 1), [(HALF, HALF), (0, 0)], precision=lax.Precision.HIGHEST)
    image = lax.conv_general_dilated(image, taps[None, None, None, :], (1, 1), [(0, 0), (HALF, HALF)], precision=lax.Precision.HIGHEST)
    return image[0, 0]

def reference(block_sums, block_weights, block_tile, block_row, prior_weight):
    total_blocks = block_sums.shape[0]
    zeros = jnp.zeros((NY, NX), jnp.float32)

    def place(index, carry):
        sums, weights = carry
        target = block_tile[index, 0].astype(jnp.int32)
        top = (target // N_TX * ROWS + block_row[index] * BAND).astype(jnp.int32)
        left = (target % N_TX * COLS).astype(jnp.int32)
        old_sums = lax.dynamic_slice(sums, (top, left), (BAND, COLS))
        old_weights = lax.dynamic_slice(weights, (top, left), (BAND, COLS))
        sums = lax.dynamic_update_slice(sums, old_sums + block_sums[index], (top, left))
        weights = lax.dynamic_update_slice(weights, old_weights + block_weights[index], (top, left))
        return (sums, weights)
    cell_sums, cell_weights = lax.fori_loop(0, total_blocks, place, (zeros, zeros))
    root = jnp.sqrt(prior_weight + cell_weights)
    right_side = cell_sums / root
    taps = kernel_taps()

    def operate(field):
        return 0.5 * field + root * smooth(root * field, taps)
    solution_field = jnp.zeros_like(right_side)
    residual, direction = (right_side, right_side)
    norm_now = jnp.sum(residual * residual)
    for step in range(ITERS):
        image = operate(direction)
        alpha = norm_now / jnp.sum(direction * image)
        solution_field = solution_field + alpha * direction
        residual = residual - alpha * image
        norm_next = jnp.sum(residual * residual)
        direction = residual + norm_next / norm_now * direction
        norm_now = norm_next
    return (solution_field, residual)
```

```python
import functools

import jax
import jax.numpy as jnp
import numpy as np
from jax import lax
from jax.experimental import pallas as pl
from jax.experimental.pallas import tpu as pltpu
from jax.sharding import PartitionSpec as P

HALF = 32
LANES = 128
MESH = pl.DeviceIdType.MESH


def taps_matrix(offset):
    def weight(distance):
        scaled = np.abs(distance) / (HALF + 1.0)
        value = (1.0 - scaled) ** 4 * (1.0 + 4.0 * scaled)
        return np.where(np.abs(distance) <= HALF, value, 0.0)

    total = np.sum(weight(np.arange(-HALF, HALF + 1).astype(np.float64)))
    return (weight(offset.astype(np.float64)) / total).astype(np.float32)


def halves(values):
    high = values.astype(jnp.bfloat16)
    return high, (values - high.astype(jnp.float32)).astype(jnp.bfloat16)


def kernel_matrices(rows, width):
    row = np.arange(rows)[:, None] - (np.arange(rows + 2 * HALF)[None, :] - HALF)
    col = (np.arange(width + 2 * LANES)[:, None] - LANES) - np.arange(width)[None, :]
    row_high, row_low = halves(jnp.asarray(taps_matrix(row)))
    col_high, col_low = halves(jnp.asarray(taps_matrix(col)))
    return jnp.concatenate([row_high, row_low], axis=0), col_high, col_low


def directions():
    return [(dy, dx) for dy in (-1, 0, 1) for dx in (-1, 0, 1) if (dy, dx) != (0, 0)]


def span(step, size, margin, width, sending):
    if step == 0:
        return pl.ds(margin, size)
    if sending:
        return pl.ds(margin, width) if step < 0 else pl.ds(margin + size - width, width)
    return pl.ds(margin + size, width) if step < 0 else pl.ds(margin - width, width)


def solve_kernel(
    ny,
    nx,
    sums_ref,
    weights_ref,
    prior_ref,
    row_ref,
    col_high_ref,
    col_low_ref,
    field_ref,
    residual_ref,
    pad_a,
    pad_b,
    part,
    parts,
    halo_send,
    halo_recv,
    part_send,
    part_recv,
):
    count = ny * nx
    rows, cols = prior_ref.shape
    width = col_high_ref.shape[1]
    ty, tx = lax.axis_index("ty"), lax.axis_index("tx")
    me = ty * nx + tx

    barrier = pltpu.get_barrier_semaphore()

    for pad in (pad_a, pad_b):
        pad[0:HALF, :] = jnp.zeros((HALF, cols + 2 * LANES), jnp.float32)
        pad[HALF + rows :, :] = jnp.zeros((HALF, cols + 2 * LANES), jnp.float32)
        pad[HALF : HALF + rows, 0:LANES] = jnp.zeros((rows, LANES), jnp.float32)
        pad[HALF : HALF + rows, LANES + cols :] = jnp.zeros((rows, LANES), jnp.float32)

    def greet(step, carry):
        other = lax.rem(me + step, count)
        pl.semaphore_signal(
            barrier, inc=1, device_id=(other // nx, lax.rem(other, nx)), device_id_type=MESH
        )
        return carry

    lax.fori_loop(1, count, greet, 0)

    pad_a[HALF : HALF + rows, LANES : LANES + cols] = sums_ref[...]
    root = jnp.sqrt(prior_ref[...] + weights_ref[...])
    pl.semaphore_wait(barrier, count - 1)

    def exchange(pad, phase):
        copies = []
        for index, (dy, dx) in enumerate(directions()):
            copy = pltpu.make_async_remote_copy(
                src_ref=pad.at[
                    span(dy, rows, HALF, HALF, True), span(dx, cols, LANES, LANES, True)
                ],
                dst_ref=pad.at[
                    span(dy, rows, HALF, HALF, False), span(dx, cols, LANES, LANES, False)
                ],
                send_sem=halo_send.at[phase, index],
                recv_sem=halo_recv.at[phase, index],
                device_id=(
                    lax.rem(ty + dy + ny, ny),
                    lax.rem(tx + dx + nx, nx),
                ),
                device_id_type=MESH,
            )
            goes = (ty + dy >= 0) & (ty + dy < ny) & (tx + dx >= 0) & (tx + dx < nx)
            comes = (ty - dy >= 0) & (ty - dy < ny) & (tx - dx >= 0) & (tx - dx < nx)
            copies.append((copy, goes, comes))
            pl.when(goes)(copy.start)
        for copy, goes, comes in copies:
            pl.when(comes)(copy.wait_recv)
        return copies

    def finish(copies):
        for copy, goes, comes in copies:
            pl.when(goes)(copy.wait_send)

    def dot(left, right):
        return jnp.dot(left, right, preferred_element_type=jnp.float32)

    def smooth(pad):
        high, low = halves(pad[...])
        both = dot(row_ref[...], high)
        down = both[:rows] + both[rows:] + dot(row_ref[0:rows, :], low)
        high, low = halves(down)
        stacked = jnp.concatenate([high, low], axis=0)
        pieces = []
        for left in range(0, cols, width):
            window = slice(left, left + width + 2 * LANES)
            both = dot(stacked[:, window], col_high_ref[...])
            pieces.append(both[:rows] + both[rows:] + dot(high[:, window], col_low_ref[...]))
        return jnp.concatenate(pieces, axis=1)

    def total(values):
        return jnp.sum(values, axis=(0, 1), keepdims=True)

    first = exchange(pad_a, 0)
    r0 = sums_ref[...] / root
    u = root * smooth(pad_a)
    pad_b[HALF : HALF + rows, LANES : LANES + cols] = root * u
    second = exchange(pad_b, 1)
    rr, ru = total(r0 * r0), total(r0 * u)
    own = jnp.where(rr > 0.0, ru / rr, 0.0)
    z = root * smooth(pad_b)
    q = own * r0 - u
    g = own * u - z
    lane = lax.broadcasted_iota(jnp.int32, (1, LANES), 1)
    packed = jnp.zeros((1, LANES), jnp.float32)
    for index, value in enumerate((rr, ru, total(q * q), total(q * g), total(r0 * g))):
        packed = jnp.where(lane == index, value, packed)
    part[...] = packed
    parts[pl.ds(me, 1), 0, :] = packed

    def tell(step, carry):
        other = lax.rem(me + step, count)
        pltpu.make_async_remote_copy(
            src_ref=part,
            dst_ref=parts.at[me],
            send_sem=part_send,
            recv_sem=part_recv,
            device_id=(other // nx, lax.rem(other, nx)),
            device_id_type=MESH,
        ).start()
        return carry

    lax.fori_loop(1, count, tell, 0)
    everyone = parts.at[pl.ds(0, count - 1)]
    pltpu.make_async_copy(everyone, everyone, part_recv).wait()

    table = parts[...].reshape(count, LANES)
    rr_d, ru_d, qq_d, qg_d, rg_d = [table[:, i : i + 1] for i in range(5)]
    rr, ru = total(rr_d), total(ru_d)
    mu = ru / rr
    shift = mu - jnp.where(rr_d > 0.0, ru_d / rr_d, 0.0)
    qq = total(qq_d + shift * shift * rr_d)
    qg = total(qg_d + shift * (rg_d - qq_d) + shift * shift * ru_d)
    alpha0 = rr / (0.5 * rr + ru)
    norm = alpha0 * alpha0 * qq
    beta = norm / rr
    alpha1 = norm / (alpha0 * alpha0 * (0.5 * qq + qg) - beta * norm / alpha0)
    q = mu * r0 - u
    r1 = alpha0 * q
    field_ref[...] = alpha0 * r0 + alpha1 * (r1 + beta * r0)
    along = alpha0 * (0.5 * q + mu * u - z) + beta * (0.5 * r0 + u)
    residual_ref[...] = r1 - alpha1 * along

    finish(first)
    finish(second)
    pltpu.make_async_copy(everyone, everyone, part_send).wait()


def solve(ny, nx, cell_sums, cell_weights, prior_weight):
    rows, cols = prior_weight.shape
    count = ny * nx
    width = 2 * LANES
    matrices = kernel_matrices(rows, width)
    vmem = pl.BlockSpec(memory_space=pltpu.VMEM)
    shape = jax.ShapeDtypeStruct((rows, cols), jnp.float32)
    padded = pltpu.VMEM((rows + 2 * HALF, cols + 2 * LANES), jnp.float32)
    return pl.pallas_call(
        functools.partial(solve_kernel, ny, nx),
        out_shape=(shape, shape),
        in_specs=[vmem] * 6,
        out_specs=(vmem, vmem),
        scratch_shapes=[
            padded,
            padded,
            pltpu.VMEM((1, LANES), jnp.float32),
            pltpu.VMEM((count, 1, LANES), jnp.float32),
            pltpu.SemaphoreType.DMA((2, 8)),
            pltpu.SemaphoreType.DMA((2, 8)),
            pltpu.SemaphoreType.DMA,
            pltpu.SemaphoreType.DMA,
        ],
        compiler_params=pltpu.CompilerParams(
            collective_id=0, has_side_effects=True, vmem_limit_bytes=40 * 2**20
        ),
    )(cell_sums, cell_weights, prior_weight, *matrices)


def shards(block_sums, block_weights, block_tile, block_row, prior_weight):
    ny, nx = lax.axis_size("ty"), lax.axis_size("tx")
    devices = ny * nx
    blocks, band, cols = block_sums.shape
    rows = prior_weight.shape[0]
    slots = 2 * blocks // devices
    target = block_tile[:, 0]
    owners = (target[:, None] == jnp.arange(devices, dtype=jnp.int32)[None, :]).astype(jnp.int32)
    rank = jnp.sum((jnp.cumsum(owners, axis=0) - 1) * owners, axis=1)
    position = target * slots + rank
    send_sums = jnp.zeros((devices * slots, band, cols), jnp.float32).at[position].set(block_sums)
    send_weights = (
        jnp.zeros((devices * slots, band, cols), jnp.float32).at[position].set(block_weights)
    )
    send_rows = jnp.zeros((devices * slots,), jnp.int32).at[position].set(block_row)

    def swap(values):
        return lax.all_to_all(values, ("ty", "tx"), split_axis=0, concat_axis=0, tiled=True)

    got_sums = swap(send_sums.reshape(devices, slots, band, cols))
    got_weights = swap(send_weights.reshape(devices, slots, band, cols))
    got_rows = swap(send_rows.reshape(devices, slots))
    received = devices * slots
    got_rows = got_rows.reshape(received)
    select = (jnp.arange(rows // band, dtype=jnp.int32)[:, None] == got_rows[None, :]).astype(
        jnp.float32
    )
    cell_sums = jnp.dot(
        select, got_sums.reshape(received, band * cols), precision=lax.Precision.HIGHEST
    )
    cell_weights = jnp.dot(
        select, got_weights.reshape(received, band * cols), precision=lax.Precision.HIGHEST
    )
    return solve(ny, nx, cell_sums, cell_weights, prior_weight)


def solution(mesh):
    in_specs = (
        P(("ty", "tx"), None, None),
        P(("ty", "tx"), None, None),
        P(("ty", "tx"), None),
        P(("ty", "tx")),
        P("ty", "tx"),
    )
    out_specs = (P("ty", "tx"), P("ty", "tx"))
    return jax.shard_map(shards, mesh=mesh, in_specs=in_specs, out_specs=out_specs, check_vma=False)
```

```python
import functools

import jax
import jax.numpy as jnp
import numpy as np
from jax import lax
from jax.experimental import pallas as pl
from jax.experimental.pallas import tpu as pltpu
from jax.sharding import PartitionSpec as P

HALF = 32
LANES = 128
MESH = pl.DeviceIdType.MESH


def taps_matrix(offset):
    def weight(distance):
        scaled = np.abs(distance) / (HALF + 1.0)
        value = (1.0 - scaled) ** 4 * (1.0 + 4.0 * scaled)
        return np.where(np.abs(distance) <= HALF, value, 0.0)

    total = np.sum(weight(np.arange(-HALF, HALF + 1).astype(np.float64)))
    return (weight(offset.astype(np.float64)) / total).astype(np.float32)


def halves(values):
    high = values.astype(jnp.bfloat16)
    return high, (values - high.astype(jnp.float32)).astype(jnp.bfloat16)


def kernel_matrices(rows, width):
    row = np.arange(rows)[:, None] - (np.arange(rows + 2 * HALF)[None, :] - HALF)
    col = (np.arange(width + 2 * LANES)[:, None] - LANES) - np.arange(width)[None, :]
    row_high, row_low = halves(jnp.asarray(taps_matrix(row)))
    col_high, col_low = halves(jnp.asarray(taps_matrix(col)))
    return jnp.concatenate([row_high, row_low], axis=0), col_high, col_low


def directions():
    return [(dy, dx) for dy in (-1, 0, 1) for dx in (-1, 0, 1) if (dy, dx) != (0, 0)]


def span(step, size, margin, width, sending):
    if step == 0:
        return pl.ds(margin, size)
    if sending:
        return pl.ds(margin, width) if step < 0 else pl.ds(margin + size - width, width)
    return pl.ds(margin + size, width) if step < 0 else pl.ds(margin - width, width)


def solve_kernel(
    ny,
    nx,
    slots,
    sums_ref,
    weights_ref,
    tile_ref,
    band_ref,
    prior_ref,
    row_ref,
    col_high_ref,
    col_low_ref,
    field_ref,
    residual_ref,
    send_sums,
    send_weights,
    send_table,
    got_sums,
    got_weights,
    got_table,
    pad_a,
    pad_b,
    part,
    parts,
    route_send,
    route_recv,
    halo_send,
    halo_recv,
    part_send,
    part_recv,
):
    count = ny * nx
    blocks, groups, _ = sums_ref.shape
    rows, cols = prior_ref.shape
    width = col_high_ref.shape[1]
    ty, tx = lax.axis_index("ty"), lax.axis_index("tx")
    me = ty * nx + tx

    barrier = pltpu.get_barrier_semaphore()

    for pad in (pad_a, pad_b):
        pad[0:HALF, :] = jnp.zeros((HALF, cols + 2 * LANES), jnp.float32)
        pad[HALF + rows :, :] = jnp.zeros((HALF, cols + 2 * LANES), jnp.float32)
        pad[HALF : HALF + rows, 0:LANES] = jnp.zeros((rows, LANES), jnp.float32)
        pad[HALF : HALF + rows, LANES + cols :] = jnp.zeros((rows, LANES), jnp.float32)

    def greet(step, carry):
        other = lax.rem(me + step, count)
        pl.semaphore_signal(
            barrier, inc=1, device_id=(other // nx, lax.rem(other, nx)), device_id_type=MESH
        )
        return carry

    lax.fori_loop(1, count, greet, 0)

    def dot(left, right):
        return jnp.dot(left, right, preferred_element_type=jnp.float32)

    def cross(left, right):
        return lax.dot_general(
            left, right, (((0,), (0,)), ((), ())), preferred_element_type=jnp.float32
        )

    def iota(shape, dim):
        return lax.broadcasted_iota(jnp.int32, shape, dim)

    def ones(mask):
        return jnp.where(mask, 1.0, 0.0).astype(jnp.bfloat16)

    tile = tile_ref[...]
    square = (blocks, blocks)
    down, across = iota(square, 0), iota(square, 1)

    def as_column(row):
        spread = jnp.broadcast_to(row, square)
        return jnp.sum(jnp.where(down == across, spread, 0), axis=1, keepdims=True)

    tile_column = as_column(tile)
    same = jnp.where(tile_column == tile, 1, 0)
    rank = jnp.sum(jnp.where(down < across, same, 0), axis=0, keepdims=True)
    rank_column = jnp.sum(jnp.where(across < down, same, 0), axis=1, keepdims=True)
    place = ones(iota((count * slots, blocks), 0) == tile * slots + rank)
    owner = ones(iota((count, blocks), 0) == tile)
    numbers = jnp.where(
        rank_column == iota((blocks, LANES), 1), as_column(band_ref[...]) + 1, 0
    ).astype(jnp.float32)
    send_table[...] = dot(owner, numbers.astype(jnp.bfloat16)).reshape(count, 1, LANES)

    def pack(source, target):
        for group in range(groups):
            high, low = halves(source[:, group, :])
            moved = dot(place, high) + dot(place, low)
            target[:, :, group * LANES : (group + 1) * LANES] = moved.reshape(count, slots, LANES)

    pack(sums_ref, send_sums)
    pack(weights_ref, send_weights)
    got_table[pl.ds(me, 1)] = send_table[pl.ds(me, 1)]
    got_sums[pl.ds(me, 1)] = send_sums[pl.ds(me, 1)]
    got_weights[pl.ds(me, 1)] = send_weights[pl.ds(me, 1)]

    pl.semaphore_wait(barrier, count - 1)

    def route(source, target, which, start, stop):
        def send(index, carry):
            hop = index // ny
            sign = 1 - 2 * lax.rem(hop, 2)
            other_x = lax.rem(tx + nx // 2 + nx + sign * ((hop + 1) // 2), nx)
            other_y = lax.rem(ty + index, ny)

            @pl.when(other_y * nx + other_x != me)
            def _():
                pltpu.make_async_remote_copy(
                    src_ref=source.at[other_y * nx + other_x],
                    dst_ref=target.at[me],
                    send_sem=route_send.at[which],
                    recv_sem=route_recv.at[which],
                    device_id=(other_y, other_x),
                    device_id_type=MESH,
                ).start()

            return carry

        lax.fori_loop(start, stop, send, 0)

    def arrived(target, which, semaphores):
        others = target.at[pl.ds(0, count - 1)]
        pltpu.make_async_copy(others, others, semaphores.at[which]).wait()

    def exchange(pad, phase):
        copies = []
        for index, (dy, dx) in enumerate(directions()):
            copy = pltpu.make_async_remote_copy(
                src_ref=pad.at[
                    span(dy, rows, HALF, HALF, True), span(dx, cols, LANES, LANES, True)
                ],
                dst_ref=pad.at[
                    span(dy, rows, HALF, HALF, False), span(dx, cols, LANES, LANES, False)
                ],
                send_sem=halo_send.at[phase, index],
                recv_sem=halo_recv.at[phase, index],
                device_id=(
                    lax.rem(ty + dy + ny, ny),
                    lax.rem(tx + dx + nx, nx),
                ),
                device_id_type=MESH,
            )
            goes = (ty + dy >= 0) & (ty + dy < ny) & (tx + dx >= 0) & (tx + dx < nx)
            comes = (ty - dy >= 0) & (ty - dy < ny) & (tx - dx >= 0) & (tx - dx < nx)
            copies.append((copy, goes, comes))
            pl.when(goes)(copy.start)
        return copies

    def receive(copies):
        for copy, goes, comes in copies:
            pl.when(comes)(copy.wait_recv)

    def finish(copies):
        for copy, goes, comes in copies:
            pl.when(goes)(copy.wait_send)

    def smooth(pad):
        high, low = halves(pad[...])
        both = dot(row_ref[...], high)
        down = both[:rows] + both[rows:] + dot(row_ref[0:rows, :], low)
        high, low = halves(down)
        stacked = jnp.concatenate([high, low], axis=0)
        pieces = []
        for left in range(0, cols, width):
            window = slice(left, left + width + 2 * LANES)
            both = dot(stacked[:, window], col_high_ref[...])
            pieces.append(both[:rows] + both[rows:] + dot(high[:, window], col_low_ref[...]))
        return jnp.concatenate(pieces, axis=1)

    def total(values):
        return jnp.sum(values, axis=(0, 1), keepdims=True)

    early = count // 2
    route(send_table, got_table, 0, 0, count)
    route(send_sums, got_sums, 1, 0, count)
    route(send_weights, got_weights, 2, 0, early)

    arrived(got_table, 0, route_recv)
    spread = ones(
        iota((count, count * slots), 0) == iota((count, count * slots), 1) // slots
    )
    table = got_table[...].reshape(count, LANES).astype(jnp.bfloat16)
    listed = cross(table, spread)
    wanted = iota(listed.shape, 0) == lax.rem(iota(listed.shape, 1), slots)
    listed = jnp.sum(jnp.where(wanted, listed, 0.0), axis=0, keepdims=True)
    select = ones(iota((rows, count * slots), 0).astype(jnp.float32) + 1.0 == listed)

    def gather(source):
        high, low = halves(source[...].reshape(count * slots, cols))
        return dot(select, high) + dot(select, low)

    arrived(got_sums, 1, route_recv)
    pad_a[HALF : HALF + rows, LANES : LANES + cols] = gather(got_sums)
    first = exchange(pad_a, 0)
    route(send_weights, got_weights, 2, early, count)
    receive(first)
    field_ref[...] = smooth(pad_a)

    arrived(got_weights, 2, route_recv)
    root = jnp.sqrt(prior_ref[...] + gather(got_weights))
    r0 = pad_a[HALF : HALF + rows, LANES : LANES + cols] / root
    u = root * field_ref[...]
    pad_b[HALF : HALF + rows, LANES : LANES + cols] = root * u
    second = exchange(pad_b, 1)
    rr, ru = total(r0 * r0), total(r0 * u)
    own = jnp.where(rr > 0.0, ru / rr, 0.0)
    receive(second)
    z = root * smooth(pad_b)
    q = own * r0 - u
    g = own * u - z
    lane = lax.broadcasted_iota(jnp.int32, (1, LANES), 1)
    packed = jnp.zeros((1, LANES), jnp.float32)
    for index, value in enumerate((rr, ru, total(q * q), total(q * g), total(r0 * g))):
        packed = jnp.where(lane == index, value, packed)
    part[...] = packed
    parts[pl.ds(me, 1), 0, :] = packed

    def tell(step, carry):
        other = lax.rem(me + step, count)
        pltpu.make_async_remote_copy(
            src_ref=part,
            dst_ref=parts.at[me],
            send_sem=part_send.at[0],
            recv_sem=part_recv.at[0],
            device_id=(other // nx, lax.rem(other, nx)),
            device_id_type=MESH,
        ).start()
        return carry

    lax.fori_loop(1, count, tell, 0)
    arrived(parts, 0, part_recv)

    table = parts[...].reshape(count, LANES)
    rr_d, ru_d, qq_d, qg_d, rg_d = [table[:, i : i + 1] for i in range(5)]
    rr, ru = total(rr_d), total(ru_d)
    mu = ru / rr
    shift = mu - jnp.where(rr_d > 0.0, ru_d / rr_d, 0.0)
    qq = total(qq_d + shift * shift * rr_d)
    qg = total(qg_d + shift * (rg_d - qq_d) + shift * shift * ru_d)
    alpha0 = rr / (0.5 * rr + ru)
    norm = alpha0 * alpha0 * qq
    beta = norm / rr
    alpha1 = norm / (alpha0 * alpha0 * (0.5 * qq + qg) - beta * norm / alpha0)
    q = mu * r0 - u
    r1 = alpha0 * q
    field_ref[...] = alpha0 * r0 + alpha1 * (r1 + beta * r0)
    along = alpha0 * (0.5 * q + mu * u - z) + beta * (0.5 * r0 + u)
    residual_ref[...] = r1 - alpha1 * along

    finish(first)
    finish(second)
    arrived(send_table, 0, route_send)
    arrived(send_sums, 1, route_send)
    arrived(send_weights, 2, route_send)
    arrived(parts, 0, part_send)


def shards(block_sums, block_weights, block_tile, block_row, prior_weight):
    ny, nx = lax.axis_size("ty"), lax.axis_size("tx")
    count = ny * nx
    blocks, band, cols = block_sums.shape
    rows = prior_weight.shape[0]
    slots = 2 * blocks // count
    matrices = kernel_matrices(rows, 2 * LANES)
    vmem = pl.BlockSpec(memory_space=pltpu.VMEM)
    shape = jax.ShapeDtypeStruct((rows, cols), jnp.float32)
    padded = pltpu.VMEM((rows + 2 * HALF, cols + 2 * LANES), jnp.float32)
    chunks = pltpu.VMEM((count, slots, cols), jnp.float32)
    lines = pltpu.VMEM((count, 1, LANES), jnp.float32)
    return pl.pallas_call(
        functools.partial(solve_kernel, ny, nx, slots),
        out_shape=(shape, shape),
        in_specs=[vmem] * 8,
        out_specs=(vmem, vmem),
        scratch_shapes=[
            chunks,
            chunks,
            lines,
            chunks,
            chunks,
            lines,
            padded,
            padded,
            pltpu.VMEM((1, LANES), jnp.float32),
            lines,
            pltpu.SemaphoreType.DMA((3,)),
            pltpu.SemaphoreType.DMA((3,)),
            pltpu.SemaphoreType.DMA((2, 8)),
            pltpu.SemaphoreType.DMA((2, 8)),
            pltpu.SemaphoreType.DMA((1,)),
            pltpu.SemaphoreType.DMA((1,)),
        ],
        compiler_params=pltpu.CompilerParams(
            collective_id=0, has_side_effects=True, vmem_limit_bytes=48 * 2**20
        ),
    )(
        block_sums.reshape(blocks * band, cols // LANES, LANES),
        block_weights.reshape(blocks * band, cols // LANES, LANES),
        block_tile.reshape(1, blocks),
        block_row.reshape(1, blocks),
        prior_weight,
        *matrices,
    )


def solution(mesh):
    in_specs = (
        P(("ty", "tx"), None, None),
        P(("ty", "tx"), None, None),
        P(("ty", "tx"), None),
        P(("ty", "tx")),
        P("ty", "tx"),
    )
    out_specs = (P("ty", "tx"), P("ty", "tx"))
    return jax.shard_map(shards, mesh=mesh, in_specs=in_specs, out_specs=out_specs, check_vma=False)
```

```python
import functools

import jax
import jax.numpy as jnp
import numpy as np
from jax import lax
from jax.experimental import pallas as pl
from jax.experimental.pallas import tpu as pltpu
from jax.sharding import PartitionSpec as P

HALF = 32
LANES = 128
PIECES = 2
MESH = pl.DeviceIdType.MESH


def taps_matrix(offset):
    def weight(distance):
        scaled = np.abs(distance) / (HALF + 1.0)
        value = (1.0 - scaled) ** 4 * (1.0 + 4.0 * scaled)
        return np.where(np.abs(distance) <= HALF, value, 0.0)

    total = np.sum(weight(np.arange(-HALF, HALF + 1).astype(np.float64)))
    return (weight(offset.astype(np.float64)) / total).astype(np.float32)


def halves(values):
    high = values.astype(jnp.bfloat16)
    return high, (values - high.astype(jnp.float32)).astype(jnp.bfloat16)


def kernel_matrices(rows, width):
    row = np.arange(rows)[:, None] - (np.arange(rows + 2 * HALF)[None, :] - HALF)
    col = (np.arange(width + 2 * LANES)[:, None] - LANES) - np.arange(width)[None, :]
    row_high, row_low = halves(jnp.asarray(taps_matrix(row)))
    col_high, col_low = halves(jnp.asarray(taps_matrix(col)))
    return jnp.concatenate([row_high, row_low], axis=0), col_high, col_low


def directions():
    return [(dy, dx) for dy in (-1, 0, 1) for dx in (-1, 0, 1) if (dy, dx) != (0, 0)]


def span(step, size, margin, width, sending):
    if step == 0:
        return pl.ds(margin, size)
    if sending:
        return pl.ds(margin, width) if step < 0 else pl.ds(margin + size - width, width)
    return pl.ds(margin + size, width) if step < 0 else pl.ds(margin - width, width)


def solve_kernel(
    ny,
    nx,
    slots,
    tile_ref,
    band_ref,
    sums_hbm,
    weights_hbm,
    prior_hbm,
    row_hbm,
    col_high_hbm,
    col_low_hbm,
    r0_ref,
    u_ref,
    z_ref,
    scalars_ref,
    sums_ref,
    weights_ref,
    prior_ref,
    row_ref,
    col_high_ref,
    col_low_ref,
    root_ref,
    load_sem,
    send_sums,
    send_weights,
    send_table,
    got_sums,
    got_weights,
    got_table,
    pad_a,
    pad_b,
    part,
    parts,
    route_send,
    route_recv,
    halo_send,
    halo_recv,
    part_send,
    part_recv,
):
    count = ny * nx
    blocks, groups, _ = sums_ref.shape
    rows, cols = prior_ref.shape
    width = col_high_ref.shape[1]
    ty, tx = lax.axis_index("ty"), lax.axis_index("tx")
    me = ty * nx + tx

    def device(index):
        hop = index // ny
        sign = 1 - 2 * lax.rem(hop, 2)
        other_x = lax.rem(tx + nx // 2 + nx + sign * ((hop + 1) // 2), nx)
        return lax.rem(ty + ny // 2 + index, ny), other_x

    barrier = pltpu.get_barrier_semaphore()

    def greet(index, carry):
        other_y, other_x = device(index)

        @pl.when(other_y * nx + other_x != me)
        def _():
            pl.semaphore_signal(
                barrier, inc=1, device_id=(other_y, other_x), device_id_type=MESH
            )

        return carry

    loads = [
        pltpu.make_async_copy(source, target, load_sem.at[index])
        for index, (source, target) in enumerate(
            (
                (sums_hbm, sums_ref),
                (weights_hbm, weights_ref),
                (row_hbm, row_ref),
                (col_high_hbm, col_high_ref),
                (col_low_hbm, col_low_ref),
                (prior_hbm, prior_ref),
            )
        )
    ]
    loads[0].start()
    loads[1].start()
    for pad in (pad_a, pad_b):
        pad[0:HALF, :] = jnp.zeros((HALF, cols + 2 * LANES), jnp.float32)
        pad[HALF + rows :, :] = jnp.zeros((HALF, cols + 2 * LANES), jnp.float32)
        pad[HALF : HALF + rows, 0:LANES] = jnp.zeros((rows, LANES), jnp.float32)
        pad[HALF : HALF + rows, LANES + cols :] = jnp.zeros((rows, LANES), jnp.float32)

    lax.fori_loop(0, count, greet, 0)
    for load in loads[2:]:
        load.start()

    def dot(left, right):
        return jnp.dot(left, right, preferred_element_type=jnp.float32)

    def cross(left, right):
        return lax.dot_general(
            left, right, (((0,), (0,)), ((), ())), preferred_element_type=jnp.float32
        )

    def iota(shape, dim):
        return lax.broadcasted_iota(jnp.int32, shape, dim)

    def ones(mask):
        return jnp.where(mask, 1.0, 0.0).astype(jnp.bfloat16)

    tile = tile_ref[...]
    square = (blocks, blocks)
    down, across = iota(square, 0), iota(square, 1)

    def as_column(row):
        spread = jnp.broadcast_to(row, square)
        return jnp.sum(jnp.where(down == across, spread, 0), axis=1, keepdims=True)

    tile_column = as_column(tile)
    same = jnp.where(tile_column == tile, 1, 0)
    rank = jnp.sum(jnp.where(down < across, same, 0), axis=0, keepdims=True)
    rank_column = jnp.sum(jnp.where(across < down, same, 0), axis=1, keepdims=True)
    place = ones(iota((count * slots, blocks), 0) == tile * slots + rank)
    owner = ones(iota((count, blocks), 0) == tile)
    numbers = jnp.where(
        rank_column == iota((blocks, LANES), 1), as_column(band_ref[...]) + 1, 0
    ).astype(jnp.float32)
    send_table[...] = dot(owner, numbers.astype(jnp.bfloat16)).reshape(count, 1, LANES)

    def pack(source, target):
        for group in range(groups):
            high, low = halves(source[:, group, :])
            moved = dot(place, high) + dot(place, low)
            target[:, :, group * LANES : (group + 1) * LANES] = moved.reshape(count, slots, LANES)

    def route(source, target, which, window=None):
        def send(index, carry):
            other_y, other_x = device(index)
            other = other_y * nx + other_x

            @pl.when(other != me)
            def _():
                pltpu.make_async_remote_copy(
                    src_ref=source.at[other] if window is None else source.at[other, :, window],
                    dst_ref=target.at[me] if window is None else target.at[me, :, window],
                    send_sem=route_send.at[which],
                    recv_sem=route_recv.at[which],
                    device_id=(other_y, other_x),
                    device_id_type=MESH,
                ).start()

            return carry

        lax.fori_loop(0, count, send, 0)

    def arrived(target, which, semaphores, window=None):
        first = pl.ds(0, count - 1)
        others = target.at[first] if window is None else target.at[first, :, window]
        pltpu.make_async_copy(others, others, semaphores.at[which]).wait()

    def exchange(pad, phase, piece=0, count_of=1):
        size = cols // count_of
        copies = []
        for index, (dy, dx) in enumerate(directions()):
            if (dx < 0 and piece > 0) or (dx > 0 and piece + 1 < count_of):
                continue
            middle = pl.ds(LANES + piece * size, size)
            copy = pltpu.make_async_remote_copy(
                src_ref=pad.at[
                    span(dy, rows, HALF, HALF, True),
                    span(dx, cols, LANES, LANES, True) if dx else middle,
                ],
                dst_ref=pad.at[
                    span(dy, rows, HALF, HALF, False),
                    span(dx, cols, LANES, LANES, False) if dx else middle,
                ],
                send_sem=halo_send.at[phase, index],
                recv_sem=halo_recv.at[phase, index],
                device_id=(
                    lax.rem(ty + dy + ny, ny),
                    lax.rem(tx + dx + nx, nx),
                ),
                device_id_type=MESH,
            )
            goes = (ty + dy >= 0) & (ty + dy < ny) & (tx + dx >= 0) & (tx + dx < nx)
            comes = (ty - dy >= 0) & (ty - dy < ny) & (tx - dx >= 0) & (tx - dx < nx)
            copies.append((copy, goes, comes))
            pl.when(goes)(copy.start)
        return copies

    def receive(copies):
        for copy, goes, comes in copies:
            pl.when(comes)(copy.wait_recv)

    def finish(copies):
        for copy, goes, comes in copies:
            pl.when(goes)(copy.wait_send)

    def smooth(pad):
        high, low = halves(pad[...])
        both = dot(row_ref[...], high)
        down = both[:rows] + both[rows:] + dot(row_ref[0:rows, :], low)
        high, low = halves(down)
        stacked = jnp.concatenate([high, low], axis=0)
        pieces = []
        for left in range(0, cols, width):
            window = slice(left, left + width + 2 * LANES)
            both = dot(stacked[:, window], col_high_ref[...])
            pieces.append(both[:rows] + both[rows:] + dot(high[:, window], col_low_ref[...]))
        return jnp.concatenate(pieces, axis=1)

    def total(values):
        return jnp.sum(values, axis=(0, 1), keepdims=True)

    size = cols // PIECES
    windows = [pl.ds(piece * size, size) for piece in range(PIECES)]
    loads[0].wait()
    pack(sums_ref, send_sums)
    pl.semaphore_wait(barrier, count - 1)
    route(send_table, got_table, 0)
    route(send_sums, got_sums, 1)
    loads[1].wait()
    pack(weights_ref, send_weights)
    route(send_weights, got_weights, 2, windows[0])
    got_table[pl.ds(me, 1)] = send_table[pl.ds(me, 1)]
    got_sums[pl.ds(me, 1)] = send_sums[pl.ds(me, 1)]
    got_weights[pl.ds(me, 1)] = send_weights[pl.ds(me, 1)]

    arrived(got_table, 0, route_recv)
    spread = ones(
        iota((count, count * slots), 0) == iota((count, count * slots), 1) // slots
    )
    table = got_table[...].reshape(count, LANES).astype(jnp.bfloat16)
    listed = cross(table, spread)
    wanted = iota(listed.shape, 0) == lax.rem(iota(listed.shape, 1), slots)
    listed = jnp.sum(jnp.where(wanted, listed, 0.0), axis=0, keepdims=True)
    select = ones(iota((rows, count * slots), 0).astype(jnp.float32) + 1.0 == listed)

    def gather(values):
        high, low = halves(values.reshape(count * slots, values.shape[-1]))
        return dot(select, high) + dot(select, low)

    arrived(got_sums, 1, route_recv)
    pad_a[HALF : HALF + rows, LANES : LANES + cols] = gather(got_sums[...])
    first = exchange(pad_a, 0)
    for piece in range(1, PIECES):
        route(send_weights, got_weights, 2 + piece, windows[piece])
    for load in loads[2:]:
        load.wait()
    receive(first)
    u_ref[...] = smooth(pad_a)

    second = []
    for piece, window in enumerate(windows):
        left = piece * size
        inner = slice(LANES + left, LANES + left + size)
        arrived(got_weights, 2 + piece, route_recv, window)
        root = jnp.sqrt(prior_ref[:, window] + gather(got_weights[:, :, window]))
        root_ref[:, window] = root
        r0_ref[:, window] = pad_a[HALF : HALF + rows, inner] / root
        u = root * u_ref[:, window]
        u_ref[:, window] = u
        pad_b[HALF : HALF + rows, inner] = root * u
        second += exchange(pad_b, 1 + piece, piece, PIECES)
    r0, u = r0_ref[...], u_ref[...]
    rr, ru = total(r0 * r0), total(r0 * u)
    own = jnp.where(rr > 0.0, ru / rr, 0.0)
    receive(second)
    z = root_ref[...] * smooth(pad_b)
    z_ref[...] = z
    q = own * r0 - u
    g = own * u - z
    lane = lax.broadcasted_iota(jnp.int32, (1, LANES), 1)
    packed = jnp.zeros((1, LANES), jnp.float32)
    for index, value in enumerate((rr, ru, total(q * q), total(q * g), total(r0 * g))):
        packed = jnp.where(lane == index, value, packed)
    part[...] = packed
    parts[pl.ds(me, 1), 0, :] = packed

    def tell(index, carry):
        other_y, other_x = device(index)

        @pl.when(other_y * nx + other_x != me)
        def _():
            pltpu.make_async_remote_copy(
                src_ref=part,
                dst_ref=parts.at[me],
                send_sem=part_send.at[0],
                recv_sem=part_recv.at[0],
                device_id=(other_y, other_x),
                device_id_type=MESH,
            ).start()

        return carry

    lax.fori_loop(0, count, tell, 0)
    arrived(parts, 0, part_recv)

    table = parts[...].reshape(count, LANES)
    rr_d, ru_d, qq_d, qg_d, rg_d = [table[:, i : i + 1] for i in range(5)]
    rr, ru = total(rr_d), total(ru_d)
    mu = ru / rr
    shift = mu - jnp.where(rr_d > 0.0, ru_d / rr_d, 0.0)
    qq = total(qq_d + shift * shift * rr_d)
    qg = total(qg_d + shift * (rg_d - qq_d) + shift * shift * ru_d)
    alpha0 = rr / (0.5 * rr + ru)
    norm = alpha0 * alpha0 * qq
    beta = norm / rr
    alpha1 = norm / (alpha0 * alpha0 * (0.5 * qq + qg) - beta * norm / alpha0)
    packed = jnp.zeros((1, LANES), jnp.float32)
    for index, value in enumerate((alpha0, alpha1, beta, mu)):
        packed = jnp.where(lane == index, value, packed)
    scalars_ref[...] = packed

    finish(first)
    finish(second)
    arrived(send_table, 0, route_send)
    arrived(send_sums, 1, route_send)
    for piece, window in enumerate(windows):
        arrived(send_weights, 2 + piece, route_send, window)
    arrived(parts, 0, part_send)


def shards(block_sums, block_weights, block_tile, block_row, prior_weight):
    ny, nx = lax.axis_size("ty"), lax.axis_size("tx")
    count = ny * nx
    blocks, band, cols = block_sums.shape
    rows = prior_weight.shape[0]
    slots = 2 * blocks // count
    matrices = kernel_matrices(rows, 2 * LANES)
    vmem = pl.BlockSpec(memory_space=pltpu.VMEM)
    shape = jax.ShapeDtypeStruct((rows, cols), jnp.float32)
    padded = pltpu.VMEM((rows + 2 * HALF, cols + 2 * LANES), jnp.float32)
    chunks = pltpu.VMEM((count, slots, cols), jnp.float32)
    lines = pltpu.VMEM((count, 1, LANES), jnp.float32)
    hbm = pl.BlockSpec(memory_space=pltpu.HBM)
    inputs = pltpu.VMEM((blocks * band, cols // LANES, LANES), jnp.float32)
    r0, u, z, scalars = pl.pallas_call(
        functools.partial(solve_kernel, ny, nx, slots),
        out_shape=(shape, shape, shape, jax.ShapeDtypeStruct((1, LANES), jnp.float32)),
        in_specs=[vmem] * 2 + [hbm] * 6,
        out_specs=(vmem,) * 4,
        scratch_shapes=[
            inputs,
            inputs,
            pltpu.VMEM((rows, cols), jnp.float32),
            *[pltpu.VMEM(matrix.shape, matrix.dtype) for matrix in matrices],
            pltpu.VMEM((rows, cols), jnp.float32),
            pltpu.SemaphoreType.DMA((6,)),
            chunks,
            chunks,
            lines,
            chunks,
            chunks,
            lines,
            padded,
            padded,
            pltpu.VMEM((1, LANES), jnp.float32),
            lines,
            pltpu.SemaphoreType.DMA((2 + PIECES,)),
            pltpu.SemaphoreType.DMA((2 + PIECES,)),
            pltpu.SemaphoreType.DMA((1 + PIECES, 8)),
            pltpu.SemaphoreType.DMA((1 + PIECES, 8)),
            pltpu.SemaphoreType.DMA((1,)),
            pltpu.SemaphoreType.DMA((1,)),
        ],
        compiler_params=pltpu.CompilerParams(
            collective_id=0, has_side_effects=True, vmem_limit_bytes=48 * 2**20
        ),
    )(
        block_tile.reshape(1, blocks),
        block_row.reshape(1, blocks),
        block_sums.reshape(blocks * band, cols // LANES, LANES),
        block_weights.reshape(blocks * band, cols // LANES, LANES),
        prior_weight,
        *matrices,
    )
    alpha0, alpha1, beta, mu = [scalars[0, index] for index in range(4)]
    q = mu * r0 - u
    r1 = alpha0 * q
    along = alpha0 * (0.5 * q + mu * u - z) + beta * (0.5 * r0 + u)
    return alpha0 * r0 + alpha1 * (r1 + beta * r0), r1 - alpha1 * along


def solution(mesh):
    in_specs = (
        P(("ty", "tx"), None, None),
        P(("ty", "tx"), None, None),
        P(("ty", "tx"), None),
        P(("ty", "tx")),
        P("ty", "tx"),
    )
    out_specs = (P("ty", "tx"), P("ty", "tx"))
    return jax.shard_map(shards, mesh=mesh, in_specs=in_specs, out_specs=out_specs, check_vma=False)
```

```python
import functools

import jax
import jax.numpy as jnp
import numpy as np
from jax import lax
from jax.experimental import pallas as pl
from jax.experimental.pallas import tpu as pltpu
from jax.sharding import PartitionSpec as P

HALF = 32
LANES = 128
PIECES = 4
LIMIT = 60 * 1024 * 1024
MESH = pl.DeviceIdType.MESH


def taps_matrix(offset):
    def weight(distance):
        scaled = np.abs(distance) / (HALF + 1.0)
        value = (1.0 - scaled) ** 4 * (1.0 + 4.0 * scaled)
        return np.where(np.abs(distance) <= HALF, value, 0.0)

    total = np.sum(weight(np.arange(-HALF, HALF + 1).astype(np.float64)))
    return (weight(offset.astype(np.float64)) / total).astype(np.float32)


def halves(values):
    high = values.astype(jnp.bfloat16)
    return high, (values - high.astype(jnp.float32)).astype(jnp.bfloat16)


def kernel_matrices(rows, width):
    row = np.arange(rows)[:, None] - (np.arange(rows + 2 * HALF)[None, :] - HALF)
    col = (np.arange(width + 2 * LANES)[:, None] - LANES) - np.arange(width)[None, :]
    row_high, row_low = halves(jnp.asarray(taps_matrix(row)))
    col_high, col_low = halves(jnp.asarray(taps_matrix(col)))
    return jnp.concatenate([row_high, row_low], axis=0), col_high, col_low


def directions():
    return [(dy, dx) for dy in (-1, 0, 1) for dx in (-1, 0, 1) if (dy, dx) != (0, 0)]


def span(step, size, margin, width, sending):
    if step == 0:
        return pl.ds(margin, size)
    if sending:
        return pl.ds(margin, width) if step < 0 else pl.ds(margin + size - width, width)
    return pl.ds(margin + size, width) if step < 0 else pl.ds(margin - width, width)


def solve_kernel(
    ny,
    nx,
    slots,
    tile_ref,
    band_ref,
    sums_hbm,
    weights_hbm,
    prior_hbm,
    row_hbm,
    col_high_hbm,
    col_low_hbm,
    field_ref,
    residual_ref,
    sums_ref,
    weights_ref,
    prior_ref,
    row_ref,
    col_high_ref,
    col_low_ref,
    root_ref,
    r0_ref,
    u_ref,
    load_sem,
    send_sums,
    send_weights,
    send_table,
    got_sums,
    got_weights,
    got_table,
    pad_a,
    pad_b,
    part,
    parts,
    route_send,
    route_recv,
    halo_send,
    halo_recv,
    part_send,
    part_recv,
):
    count = ny * nx
    blocks, groups, _ = sums_ref.shape
    rows, cols = prior_ref.shape
    width = col_high_ref.shape[1]
    ty, tx = lax.axis_index("ty"), lax.axis_index("tx")
    me = ty * nx + tx

    def device(index):
        hop = index // ny
        sign = 1 - 2 * lax.rem(hop, 2)
        other_x = lax.rem(tx + nx // 2 + nx + sign * ((hop + 1) // 2), nx)
        return lax.rem(ty + ny // 2 + index, ny), other_x

    barrier = pltpu.get_barrier_semaphore()

    def greet(index, carry):
        other_y, other_x = device(index)

        @pl.when(other_y * nx + other_x != me)
        def _():
            pl.semaphore_signal(
                barrier, inc=1, device_id=(other_y, other_x), device_id_type=MESH
            )

        return carry

    loads = [
        pltpu.make_async_copy(source, target, load_sem.at[index])
        for index, (source, target) in enumerate(
            (
                (sums_hbm, sums_ref),
                (weights_hbm, weights_ref),
                (row_hbm, row_ref),
                (col_high_hbm, col_high_ref),
                (col_low_hbm, col_low_ref),
                (prior_hbm, prior_ref),
            )
        )
    ]
    loads[0].start()
    loads[1].start()
    for pad in (pad_a, pad_b):
        pad[0:HALF, :] = jnp.zeros((HALF, cols + 2 * LANES), jnp.float32)
        pad[HALF + rows :, :] = jnp.zeros((HALF, cols + 2 * LANES), jnp.float32)
        pad[HALF : HALF + rows, 0:LANES] = jnp.zeros((rows, LANES), jnp.float32)
        pad[HALF : HALF + rows, LANES + cols :] = jnp.zeros((rows, LANES), jnp.float32)

    lax.fori_loop(0, count, greet, 0)
    for load in loads[2:]:
        load.start()

    def dot(left, right):
        return jnp.dot(left, right, preferred_element_type=jnp.float32)

    def cross(left, right):
        return lax.dot_general(
            left, right, (((0,), (0,)), ((), ())), preferred_element_type=jnp.float32
        )

    def iota(shape, dim):
        return lax.broadcasted_iota(jnp.int32, shape, dim)

    def ones(mask):
        return jnp.where(mask, 1.0, 0.0).astype(jnp.bfloat16)

    tile = tile_ref[...]
    square = (blocks, blocks)
    down, across = iota(square, 0), iota(square, 1)

    def as_column(row):
        spread = jnp.broadcast_to(row, square)
        return jnp.sum(jnp.where(down == across, spread, 0), axis=1, keepdims=True)

    tile_column = as_column(tile)
    same = jnp.where(tile_column == tile, 1, 0)
    rank = jnp.sum(jnp.where(down < across, same, 0), axis=0, keepdims=True)
    rank_column = jnp.sum(jnp.where(across < down, same, 0), axis=1, keepdims=True)
    place = ones(iota((count * slots, blocks), 0) == tile * slots + rank)
    owner = ones(iota((count, blocks), 0) == tile)
    numbers = jnp.where(
        rank_column == iota((blocks, LANES), 1), as_column(band_ref[...]) + 1, 0
    ).astype(jnp.float32)
    send_table[...] = dot(owner, numbers.astype(jnp.bfloat16)).reshape(count, 1, LANES)

    def pack(source, target):
        for group in range(groups):
            high, low = halves(source[:, group, :])
            moved = dot(place, high) + dot(place, low)
            target[:, :, group * LANES : (group + 1) * LANES] = moved.reshape(count, slots, LANES)

    def route(source, target, which, window=None):
        def send(index, carry):
            other_y, other_x = device(index)
            other = other_y * nx + other_x

            @pl.when(other != me)
            def _():
                pltpu.make_async_remote_copy(
                    src_ref=source.at[other] if window is None else source.at[other, :, window],
                    dst_ref=target.at[me] if window is None else target.at[me, :, window],
                    send_sem=route_send.at[which],
                    recv_sem=route_recv.at[which],
                    device_id=(other_y, other_x),
                    device_id_type=MESH,
                ).start()

            return carry

        lax.fori_loop(0, count, send, 0)

    def arrived(target, which, semaphores, window=None):
        first = pl.ds(0, count - 1)
        others = target.at[first] if window is None else target.at[first, :, window]
        pltpu.make_async_copy(others, others, semaphores.at[which]).wait()

    def exchange(pad, phase, piece=0, count_of=1):
        size = cols // count_of
        copies = []
        for index, (dy, dx) in enumerate(directions()):
            if (dx < 0 and piece > 0) or (dx > 0 and piece + 1 < count_of):
                continue
            middle = pl.ds(LANES + piece * size, size)
            copy = pltpu.make_async_remote_copy(
                src_ref=pad.at[
                    span(dy, rows, HALF, HALF, True),
                    span(dx, cols, LANES, LANES, True) if dx else middle,
                ],
                dst_ref=pad.at[
                    span(dy, rows, HALF, HALF, False),
                    span(dx, cols, LANES, LANES, False) if dx else middle,
                ],
                send_sem=halo_send.at[phase, index],
                recv_sem=halo_recv.at[phase, index],
                device_id=(
                    lax.rem(ty + dy + ny, ny),
                    lax.rem(tx + dx + nx, nx),
                ),
                device_id_type=MESH,
            )
            goes = (ty + dy >= 0) & (ty + dy < ny) & (tx + dx >= 0) & (tx + dx < nx)
            comes = (ty - dy >= 0) & (ty - dy < ny) & (tx - dx >= 0) & (tx - dx < nx)
            copies.append((copy, goes, comes))
            pl.when(goes)(copy.start)
        return copies

    def receive(copies):
        for copy, goes, comes in copies:
            pl.when(comes)(copy.wait_recv)

    def finish(copies):
        for copy, goes, comes in copies:
            pl.when(goes)(copy.wait_send)

    def smooth(pad):
        high, low = halves(pad[...])
        both = dot(row_ref[...], high)
        down = both[:rows] + both[rows:] + dot(row_ref[0:rows, :], low)
        high, low = halves(down)
        stacked = jnp.concatenate([high, low], axis=0)
        pieces = []
        for left in range(0, cols, width):
            window = slice(left, left + width + 2 * LANES)
            both = dot(stacked[:, window], col_high_ref[...])
            pieces.append(both[:rows] + both[rows:] + dot(high[:, window], col_low_ref[...]))
        return jnp.concatenate(pieces, axis=1)

    def total(values):
        return jnp.sum(values, axis=(0, 1), keepdims=True)

    size = cols // PIECES
    windows = [pl.ds(piece * size, size) for piece in range(PIECES)]
    loads[0].wait()
    pack(sums_ref, send_sums)
    pl.semaphore_wait(barrier, count - 1)
    route(send_table, got_table, 0)
    route(send_sums, got_sums, 1)
    loads[1].wait()
    pack(weights_ref, send_weights)
    route(send_weights, got_weights, 2, windows[0])
    got_table[pl.ds(me, 1)] = send_table[pl.ds(me, 1)]
    got_sums[pl.ds(me, 1)] = send_sums[pl.ds(me, 1)]
    got_weights[pl.ds(me, 1)] = send_weights[pl.ds(me, 1)]

    arrived(got_table, 0, route_recv)
    spread = ones(
        iota((count, count * slots), 0) == iota((count, count * slots), 1) // slots
    )
    table = got_table[...].reshape(count, LANES).astype(jnp.bfloat16)
    listed = cross(table, spread)
    wanted = iota(listed.shape, 0) == lax.rem(iota(listed.shape, 1), slots)
    listed = jnp.sum(jnp.where(wanted, listed, 0.0), axis=0, keepdims=True)
    select = ones(iota((rows, count * slots), 0).astype(jnp.float32) + 1.0 == listed)

    def gather(values):
        high, low = halves(values.reshape(count * slots, values.shape[-1]))
        return dot(select, high) + dot(select, low)

    arrived(got_sums, 1, route_recv)
    pad_a[HALF : HALF + rows, LANES : LANES + cols] = gather(got_sums[...])
    first = exchange(pad_a, 0)
    for piece in range(1, PIECES):
        route(send_weights, got_weights, 2 + piece, windows[piece])
    for load in loads[2:]:
        load.wait()
    receive(first)
    u_ref[...] = smooth(pad_a)

    second = []
    for piece, window in enumerate(windows):
        left = piece * size
        inner = slice(LANES + left, LANES + left + size)
        arrived(got_weights, 2 + piece, route_recv, window)
        root = jnp.sqrt(prior_ref[:, window] + gather(got_weights[:, :, window]))
        root_ref[:, window] = root
        r0_ref[:, window] = pad_a[HALF : HALF + rows, inner] / root
        u = root * u_ref[:, window]
        u_ref[:, window] = u
        pad_b[HALF : HALF + rows, inner] = root * u
        second += exchange(pad_b, 1 + piece, piece, PIECES)
    r0, u = r0_ref[...], u_ref[...]
    rr, ru = total(r0 * r0), total(r0 * u)
    own = jnp.where(rr > 0.0, ru / rr, 0.0)
    receive(second)
    z = root_ref[...] * smooth(pad_b)
    q = own * r0 - u
    g = own * u - z
    lane = lax.broadcasted_iota(jnp.int32, (1, LANES), 1)
    packed = jnp.zeros((1, LANES), jnp.float32)
    for index, value in enumerate((rr, ru, total(q * q), total(q * g), total(r0 * g))):
        packed = jnp.where(lane == index, value, packed)
    part[...] = packed
    parts[pl.ds(me, 1), 0, :] = packed

    def tell(index, carry):
        other_y, other_x = device(index)

        @pl.when(other_y * nx + other_x != me)
        def _():
            pltpu.make_async_remote_copy(
                src_ref=part,
                dst_ref=parts.at[me],
                send_sem=part_send.at[0],
                recv_sem=part_recv.at[0],
                device_id=(other_y, other_x),
                device_id_type=MESH,
            ).start()

        return carry

    lax.fori_loop(0, count, tell, 0)
    arrived(parts, 0, part_recv)

    table = parts[...].reshape(count, LANES)
    rr_d, ru_d, qq_d, qg_d, rg_d = [table[:, i : i + 1] for i in range(5)]
    rr, ru = total(rr_d), total(ru_d)
    mu = ru / rr
    shift = mu - jnp.where(rr_d > 0.0, ru_d / rr_d, 0.0)
    qq = total(qq_d + shift * shift * rr_d)
    qg = total(qg_d + shift * (rg_d - qq_d) + shift * shift * ru_d)
    alpha0 = rr / (0.5 * rr + ru)
    norm = alpha0 * alpha0 * qq
    beta = norm / rr
    alpha1 = norm / (alpha0 * alpha0 * (0.5 * qq + qg) - beta * norm / alpha0)
    q = mu * r0 - u
    r1 = alpha0 * q
    field_ref[...] = alpha0 * r0 + alpha1 * (r1 + beta * r0)
    along = alpha0 * (0.5 * q + mu * u - z) + beta * (0.5 * r0 + u)
    residual_ref[...] = r1 - alpha1 * along

    finish(first)
    finish(second)
    arrived(send_table, 0, route_send)
    arrived(send_sums, 1, route_send)
    for piece, window in enumerate(windows):
        arrived(send_weights, 2 + piece, route_send, window)
    arrived(parts, 0, part_send)


def shards(block_sums, block_weights, block_tile, block_row, prior_weight):
    ny, nx = lax.axis_size("ty"), lax.axis_size("tx")
    count = ny * nx
    blocks, band, cols = block_sums.shape
    rows = prior_weight.shape[0]
    slots = 2 * blocks // count
    matrices = kernel_matrices(rows, 2 * LANES)
    vmem = pl.BlockSpec(memory_space=pltpu.VMEM)
    shape = jax.ShapeDtypeStruct((rows, cols), jnp.float32)
    padded = pltpu.VMEM((rows + 2 * HALF, cols + 2 * LANES), jnp.float32)
    chunks = pltpu.VMEM((count, slots, cols), jnp.float32)
    lines = pltpu.VMEM((count, 1, LANES), jnp.float32)
    hbm = pl.BlockSpec(memory_space=pltpu.HBM)
    inputs = pltpu.VMEM((blocks * band, cols // LANES, LANES), jnp.float32)
    return pl.pallas_call(
        functools.partial(solve_kernel, ny, nx, slots),
        out_shape=(shape, shape),
        in_specs=[vmem] * 2 + [hbm] * 6,
        out_specs=(vmem,) * 2,
        scratch_shapes=[
            inputs,
            inputs,
            pltpu.VMEM((rows, cols), jnp.float32),
            *[pltpu.VMEM(matrix.shape, matrix.dtype) for matrix in matrices],
            pltpu.VMEM((rows, cols), jnp.float32),
            pltpu.VMEM((rows, cols), jnp.float32),
            pltpu.VMEM((rows, cols), jnp.float32),
            pltpu.SemaphoreType.DMA((6,)),
            chunks,
            chunks,
            lines,
            chunks,
            chunks,
            lines,
            padded,
            padded,
            pltpu.VMEM((1, LANES), jnp.float32),
            lines,
            pltpu.SemaphoreType.DMA((2 + PIECES,)),
            pltpu.SemaphoreType.DMA((2 + PIECES,)),
            pltpu.SemaphoreType.DMA((1 + PIECES, 8)),
            pltpu.SemaphoreType.DMA((1 + PIECES, 8)),
            pltpu.SemaphoreType.DMA((1,)),
            pltpu.SemaphoreType.DMA((1,)),
        ],
        compiler_params=pltpu.CompilerParams(
            collective_id=0, has_side_effects=True, vmem_limit_bytes=LIMIT
        ),
    )(
        block_tile.reshape(1, blocks),
        block_row.reshape(1, blocks),
        block_sums.reshape(blocks * band, cols // LANES, LANES),
        block_weights.reshape(blocks * band, cols // LANES, LANES),
        prior_weight,
        *matrices,
    )


def solution(mesh):
    in_specs = (
        P(("ty", "tx"), None, None),
        P(("ty", "tx"), None, None),
        P(("ty", "tx"), None),
        P(("ty", "tx")),
        P("ty", "tx"),
    )
    out_specs = (P("ty", "tx"), P("ty", "tx"))
    return jax.shard_map(shards, mesh=mesh, in_specs=in_specs, out_specs=out_specs, check_vma=False)
```

```python
import functools

import jax
import jax.numpy as jnp
import numpy as np
from jax import lax
from jax.experimental import pallas as pl
from jax.experimental.pallas import tpu as pltpu
from jax.sharding import PartitionSpec as P

HALF = 32
LANES = 128
PIECES = 8
LIMIT = 60 * 1024 * 1024
MESH = pl.DeviceIdType.MESH


def taps_matrix(offset):
    def weight(distance):
        scaled = np.abs(distance) / (HALF + 1.0)
        value = (1.0 - scaled) ** 4 * (1.0 + 4.0 * scaled)
        return np.where(np.abs(distance) <= HALF, value, 0.0)

    total = np.sum(weight(np.arange(-HALF, HALF + 1).astype(np.float64)))
    return (weight(offset.astype(np.float64)) / total).astype(np.float32)


def halves(values):
    high = values.astype(jnp.bfloat16)
    return high, (values - high.astype(jnp.float32)).astype(jnp.bfloat16)


def kernel_matrices(rows, width):
    row = np.arange(rows)[:, None] - (np.arange(rows + 2 * HALF)[None, :] - HALF)
    col = (np.arange(width + 2 * LANES)[:, None] - LANES) - np.arange(width)[None, :]
    row_high, row_low = halves(jnp.asarray(taps_matrix(row)))
    col_high, col_low = halves(jnp.asarray(taps_matrix(col)))
    return jnp.concatenate([row_high, row_low], axis=0), col_high, col_low


def directions():
    return [(dy, dx) for dy in (-1, 0, 1) for dx in (-1, 0, 1) if (dy, dx) != (0, 0)]


def span(step, size, margin, width, sending):
    if step == 0:
        return pl.ds(margin, size)
    if sending:
        return pl.ds(margin, width) if step < 0 else pl.ds(margin + size - width, width)
    return pl.ds(margin + size, width) if step < 0 else pl.ds(margin - width, width)


def solve_kernel(
    ny,
    nx,
    slots,
    tile_ref,
    band_ref,
    sums_hbm,
    weights_hbm,
    prior_hbm,
    row_hbm,
    col_high_hbm,
    col_low_hbm,
    field_ref,
    residual_ref,
    sums_ref,
    weights_ref,
    prior_ref,
    row_ref,
    col_high_ref,
    col_low_ref,
    root_ref,
    r0_ref,
    u_ref,
    load_sem,
    send_sums,
    send_weights,
    send_table,
    got_sums,
    got_weights,
    got_table,
    pad_a,
    pad_b,
    part,
    parts,
    route_send,
    route_recv,
    halo_send,
    halo_recv,
    part_send,
    part_recv,
):
    count = ny * nx
    blocks, groups, _ = sums_ref.shape
    rows, cols = prior_ref.shape
    width = col_high_ref.shape[1]
    ty, tx = lax.axis_index("ty"), lax.axis_index("tx")
    me = ty * nx + tx

    def device(index):
        hop = index // ny
        sign = 1 - 2 * lax.rem(hop, 2)
        other_x = lax.rem(tx + nx // 2 + nx + sign * ((hop + 1) // 2), nx)
        return lax.rem(ty + ny // 2 + index, ny), other_x

    barrier = pltpu.get_barrier_semaphore()

    def greet(index, carry):
        other_y, other_x = device(index)

        @pl.when(other_y * nx + other_x != me)
        def _():
            pl.semaphore_signal(
                barrier, inc=1, device_id=(other_y, other_x), device_id_type=MESH
            )

        return carry

    loads = [
        pltpu.make_async_copy(source, target, load_sem.at[index])
        for index, (source, target) in enumerate(
            (
                (sums_hbm, sums_ref),
                (weights_hbm, weights_ref),
                (row_hbm, row_ref),
                (col_high_hbm, col_high_ref),
                (col_low_hbm, col_low_ref),
                (prior_hbm, prior_ref),
            )
        )
    ]
    loads[0].start()
    loads[1].start()
    for pad in (pad_a, pad_b):
        pad[0:HALF, :] = jnp.zeros((HALF, cols + 2 * LANES), jnp.float32)
        pad[HALF + rows :, :] = jnp.zeros((HALF, cols + 2 * LANES), jnp.float32)
        pad[HALF : HALF + rows, 0:LANES] = jnp.zeros((rows, LANES), jnp.float32)
        pad[HALF : HALF + rows, LANES + cols :] = jnp.zeros((rows, LANES), jnp.float32)

    lax.fori_loop(0, count, greet, 0)
    for load in loads[2:]:
        load.start()

    def dot(left, right):
        return jnp.dot(left, right, preferred_element_type=jnp.float32)

    def cross(left, right):
        return lax.dot_general(
            left, right, (((0,), (0,)), ((), ())), preferred_element_type=jnp.float32
        )

    def iota(shape, dim):
        return lax.broadcasted_iota(jnp.int32, shape, dim)

    def ones(mask):
        return jnp.where(mask, 1.0, 0.0).astype(jnp.bfloat16)

    tile = tile_ref[...]
    square = (blocks, blocks)
    down, across = iota(square, 0), iota(square, 1)

    def as_column(row):
        spread = jnp.broadcast_to(row, square)
        return jnp.sum(jnp.where(down == across, spread, 0), axis=1, keepdims=True)

    tile_column = as_column(tile)
    same = jnp.where(tile_column == tile, 1, 0)
    rank = jnp.sum(jnp.where(down < across, same, 0), axis=0, keepdims=True)
    rank_column = jnp.sum(jnp.where(across < down, same, 0), axis=1, keepdims=True)
    place = ones(iota((count * slots, blocks), 0) == tile * slots + rank)
    owner = ones(iota((count, blocks), 0) == tile)
    numbers = jnp.where(
        rank_column == iota((blocks, LANES), 1), as_column(band_ref[...]) + 1, 0
    ).astype(jnp.float32)
    send_table[...] = dot(owner, numbers.astype(jnp.bfloat16)).reshape(count, 1, LANES)

    def pack(source, target):
        for group in range(groups):
            high, low = halves(source[:, group, :])
            moved = dot(place, high) + dot(place, low)
            target[:, :, group * LANES : (group + 1) * LANES] = moved.reshape(count, slots, LANES)

    def route(source, target, which, window=None):
        def send(index, carry):
            other_y, other_x = device(index)
            other = other_y * nx + other_x

            @pl.when(other != me)
            def _():
                pltpu.make_async_remote_copy(
                    src_ref=source.at[other] if window is None else source.at[other, :, window],
                    dst_ref=target.at[me] if window is None else target.at[me, :, window],
                    send_sem=route_send.at[which],
                    recv_sem=route_recv.at[which],
                    device_id=(other_y, other_x),
                    device_id_type=MESH,
                ).start()

            return carry

        lax.fori_loop(0, count, send, 0)

    def arrived(target, which, semaphores, window=None):
        first = pl.ds(0, count - 1)
        others = target.at[first] if window is None else target.at[first, :, window]
        pltpu.make_async_copy(others, others, semaphores.at[which]).wait()

    def exchange(pad, phase, piece=0, count_of=1):
        size = cols // count_of
        copies = []
        for index, (dy, dx) in enumerate(directions()):
            if (dx < 0 and piece > 0) or (dx > 0 and piece + 1 < count_of):
                continue
            middle = pl.ds(LANES + piece * size, size)
            copy = pltpu.make_async_remote_copy(
                src_ref=pad.at[
                    span(dy, rows, HALF, HALF, True),
                    span(dx, cols, LANES, LANES, True) if dx else middle,
                ],
                dst_ref=pad.at[
                    span(dy, rows, HALF, HALF, False),
                    span(dx, cols, LANES, LANES, False) if dx else middle,
                ],
                send_sem=halo_send.at[phase, index],
                recv_sem=halo_recv.at[phase, index],
                device_id=(
                    lax.rem(ty + dy + ny, ny),
                    lax.rem(tx + dx + nx, nx),
                ),
                device_id_type=MESH,
            )
            goes = (ty + dy >= 0) & (ty + dy < ny) & (tx + dx >= 0) & (tx + dx < nx)
            comes = (ty - dy >= 0) & (ty - dy < ny) & (tx - dx >= 0) & (tx - dx < nx)
            copies.append((copy, goes, comes))
            pl.when(goes)(copy.start)
        return copies

    def receive(copies):
        for copy, goes, comes in copies:
            pl.when(comes)(copy.wait_recv)

    def finish(copies):
        for copy, goes, comes in copies:
            pl.when(goes)(copy.wait_send)

    def smooth(pad):
        high, low = halves(pad[...])
        both = dot(row_ref[...], high)
        down = both[:rows] + both[rows:] + dot(row_ref[0:rows, :], low)
        high, low = halves(down)
        stacked = jnp.concatenate([high, low], axis=0)
        pieces = []
        for left in range(0, cols, width):
            window = slice(left, left + width + 2 * LANES)
            both = dot(stacked[:, window], col_high_ref[...])
            pieces.append(both[:rows] + both[rows:] + dot(high[:, window], col_low_ref[...]))
        return jnp.concatenate(pieces, axis=1)

    def total(values):
        return jnp.sum(values, axis=(0, 1), keepdims=True)

    size = cols // PIECES
    windows = [pl.ds(piece * size, size) for piece in range(PIECES)]
    loads[0].wait()
    pack(sums_ref, send_sums)
    pl.semaphore_wait(barrier, count - 1)
    route(send_table, got_table, 0)
    route(send_sums, got_sums, 1)
    loads[1].wait()
    pack(weights_ref, send_weights)
    route(send_weights, got_weights, 2, windows[0])
    got_table[pl.ds(me, 1)] = send_table[pl.ds(me, 1)]
    got_sums[pl.ds(me, 1)] = send_sums[pl.ds(me, 1)]
    got_weights[pl.ds(me, 1)] = send_weights[pl.ds(me, 1)]

    arrived(got_table, 0, route_recv)
    spread = ones(
        iota((count, count * slots), 0) == iota((count, count * slots), 1) // slots
    )
    table = got_table[...].reshape(count, LANES).astype(jnp.bfloat16)
    listed = cross(table, spread)
    wanted = iota(listed.shape, 0) == lax.rem(iota(listed.shape, 1), slots)
    listed = jnp.sum(jnp.where(wanted, listed, 0.0), axis=0, keepdims=True)
    select = ones(iota((rows, count * slots), 0).astype(jnp.float32) + 1.0 == listed)

    def gather(values):
        high, low = halves(values.reshape(count * slots, values.shape[-1]))
        return dot(select, high) + dot(select, low)

    arrived(got_sums, 1, route_recv)
    pad_a[HALF : HALF + rows, LANES : LANES + cols] = gather(got_sums[...])
    first = exchange(pad_a, 0)
    for piece in range(1, PIECES):
        route(send_weights, got_weights, 2 + piece, windows[piece])
    for load in loads[2:]:
        load.wait()
    receive(first)
    u_ref[...] = smooth(pad_a)

    second = []
    for piece, window in enumerate(windows):
        left = piece * size
        inner = slice(LANES + left, LANES + left + size)
        arrived(got_weights, 2 + piece, route_recv, window)
        root = jnp.sqrt(prior_ref[:, window] + gather(got_weights[:, :, window]))
        root_ref[:, window] = root
        r0_ref[:, window] = pad_a[HALF : HALF + rows, inner] / root
        u = root * u_ref[:, window]
        u_ref[:, window] = u
        pad_b[HALF : HALF + rows, inner] = root * u
        second += exchange(pad_b, 1 + piece, piece, PIECES)
    r0, u = r0_ref[...], u_ref[...]
    rr, ru = total(r0 * r0), total(r0 * u)
    own = jnp.where(rr > 0.0, ru / rr, 0.0)
    receive(second)
    z = root_ref[...] * smooth(pad_b)
    q = own * r0 - u
    g = own * u - z
    lane = lax.broadcasted_iota(jnp.int32, (1, LANES), 1)
    packed = jnp.zeros((1, LANES), jnp.float32)
    for index, value in enumerate((rr, ru, total(q * q), total(q * g), total(r0 * g))):
        packed = jnp.where(lane == index, value, packed)
    part[...] = packed
    parts[pl.ds(me, 1), 0, :] = packed

    def tell(index, carry):
        other_y, other_x = device(index)

        @pl.when(other_y * nx + other_x != me)
        def _():
            pltpu.make_async_remote_copy(
                src_ref=part,
                dst_ref=parts.at[me],
                send_sem=part_send.at[0],
                recv_sem=part_recv.at[0],
                device_id=(other_y, other_x),
                device_id_type=MESH,
            ).start()

        return carry

    lax.fori_loop(0, count, tell, 0)
    arrived(parts, 0, part_recv)

    table = parts[...].reshape(count, LANES)
    rr_d, ru_d, qq_d, qg_d, rg_d = [table[:, i : i + 1] for i in range(5)]
    rr, ru = total(rr_d), total(ru_d)
    mu = ru / rr
    shift = mu - jnp.where(rr_d > 0.0, ru_d / rr_d, 0.0)
    qq = total(qq_d + shift * shift * rr_d)
    qg = total(qg_d + shift * (rg_d - qq_d) + shift * shift * ru_d)
    alpha0 = rr / (0.5 * rr + ru)
    norm = alpha0 * alpha0 * qq
    beta = norm / rr
    alpha1 = norm / (alpha0 * alpha0 * (0.5 * qq + qg) - beta * norm / alpha0)
    q = mu * r0 - u
    r1 = alpha0 * q
    field_ref[...] = alpha0 * r0 + alpha1 * (r1 + beta * r0)
    along = alpha0 * (0.5 * q + mu * u - z) + beta * (0.5 * r0 + u)
    residual_ref[...] = r1 - alpha1 * along

    finish(first)
    finish(second)
    arrived(send_table, 0, route_send)
    arrived(send_sums, 1, route_send)
    for piece, window in enumerate(windows):
        arrived(send_weights, 2 + piece, route_send, window)
    arrived(parts, 0, part_send)


def shards(block_sums, block_weights, block_tile, block_row, prior_weight):
    ny, nx = lax.axis_size("ty"), lax.axis_size("tx")
    count = ny * nx
    blocks, band, cols = block_sums.shape
    rows = prior_weight.shape[0]
    slots = 2 * blocks // count
    matrices = kernel_matrices(rows, 2 * LANES)
    vmem = pl.BlockSpec(memory_space=pltpu.VMEM)
    shape = jax.ShapeDtypeStruct((rows, cols), jnp.float32)
    padded = pltpu.VMEM((rows + 2 * HALF, cols + 2 * LANES), jnp.float32)
    chunks = pltpu.VMEM((count, slots, cols), jnp.float32)
    lines = pltpu.VMEM((count, 1, LANES), jnp.float32)
    hbm = pl.BlockSpec(memory_space=pltpu.HBM)
    inputs = pltpu.VMEM((blocks * band, cols // LANES, LANES), jnp.float32)
    return pl.pallas_call(
        functools.partial(solve_kernel, ny, nx, slots),
        out_shape=(shape, shape),
        in_specs=[vmem] * 2 + [hbm] * 6,
        out_specs=(vmem,) * 2,
        scratch_shapes=[
            inputs,
            inputs,
            pltpu.VMEM((rows, cols), jnp.float32),
            *[pltpu.VMEM(matrix.shape, matrix.dtype) for matrix in matrices],
            pltpu.VMEM((rows, cols), jnp.float32),
            pltpu.VMEM((rows, cols), jnp.float32),
            pltpu.VMEM((rows, cols), jnp.float32),
            pltpu.SemaphoreType.DMA((6,)),
            chunks,
            chunks,
            lines,
            chunks,
            chunks,
            lines,
            padded,
            padded,
            pltpu.VMEM((1, LANES), jnp.float32),
            lines,
            pltpu.SemaphoreType.DMA((2 + PIECES,)),
            pltpu.SemaphoreType.DMA((2 + PIECES,)),
            pltpu.SemaphoreType.DMA((1 + PIECES, 8)),
            pltpu.SemaphoreType.DMA((1 + PIECES, 8)),
            pltpu.SemaphoreType.DMA((1,)),
            pltpu.SemaphoreType.DMA((1,)),
        ],
        compiler_params=pltpu.CompilerParams(
            collective_id=0, has_side_effects=True, vmem_limit_bytes=LIMIT
        ),
    )(
        block_tile.reshape(1, blocks),
        block_row.reshape(1, blocks),
        block_sums.reshape(blocks * band, cols // LANES, LANES),
        block_weights.reshape(blocks * band, cols // LANES, LANES),
        prior_weight,
        *matrices,
    )


def solution(mesh):
    in_specs = (
        P(("ty", "tx"), None, None),
        P(("ty", "tx"), None, None),
        P(("ty", "tx"), None),
        P(("ty", "tx")),
        P("ty", "tx"),
    )
    out_specs = (P("ty", "tx"), P("ty", "tx"))
    return jax.shard_map(shards, mesh=mesh, in_specs=in_specs, out_specs=out_specs, check_vma=False)
```
